256 devices in a mesh: section: 2 (over core), expert: 32 (over z, x), dp: 4 (over y).
Axes of the slice: x: 4, y: 4, z: 8, core: 2. Of those that a mesh axis runs over, the one named last changes fastest.
Arguments:
- layer_inputs: bfloat16 [2, 4096, 2048], P('section', 'expert'), may hold values from -6 to 6
- out_grad: bfloat16 [4096, 2048], P('expert'), may hold values from -6 to 6
- expert_ids: int32 [2, 4096, 6], P('section', 'expert'), may hold values from 0 to 63, all different within a row; in each aligned block of 128 rows (0 to 127, 128 to 255, ..., all dimensions but the last counted through in order) at most 16 rows name the same one
- gate_weights: float32 [2, 4096, 6], P('section', 'expert'), may hold values from 0.05 to 0.5
- w_gate: bfloat16 [2, 64, 2048, 1408], P('section', 'expert', None, 'dp'), may hold values from -0.125 to 0.125
- w_up: bfloat16 [2, 64, 2048, 1408], P('section', 'expert', None, 'dp'), may hold values from -0.125 to 0.125
- w_down: bfloat16 [2, 64, 1408, 2048], P('section', 'expert', 'dp'), may hold values from -0.15625 to 0.15625
Outputs:
- input_grads: bfloat16 [2, 4096, 2048], P('section', 'expert')
The draws below stay inside these ranges and needn't reach their ends.
Inputs may be any that keep to these rules, and one draw needn't show every extreme that they name: `expert_ids`: each row names 6 different experts. In the 128 rows of one index of expert, no expert of a layer is named by more than 16 rows, a bound that some block reaches.
All inputs are finite; a program needn't handle non-finite values.
Results may differ from the reference program's by a relative error of at most 0.006.
Values may be sent and summed in bfloat16 or wider, within the bound.
A program may use at most 128 MiB of HBM per device.

```python
import math
import jax
import jax.numpy as jnp
import numpy as np
from jax import lax

D = 2048
FF = 1408
TOP = 6
TOK_DEV = 128
EXPERTS = 64
LAYERS = 2
TOKENS = 4096
CAP = 16
N_EXPERT = 32
N_DP = 4


def levels(rng, shape, shards, smallest, high):
    def one(dim, parts):
        draws = jax.random.uniform(jax.random.fold_in(jax.random.fold_in(rng, 6), dim), (parts,), jnp.float32, smallest / len(shards), high / len(shards))
        return jnp.repeat(jnp.exp(draws), shape[dim] // parts).reshape((-1,) + (1,) * (len(shape) - dim - 1))

    level = one(*shards[0])
    for cut in shards[1:]:
        level = level * one(*cut)
    return level


def assign_block(stream_key, own, number, rows, amount, top, limit, skew):
    order = jax.random.permutation(stream_key, amount)
    crowded, common = portions_of(amount, rows * top, limit, skew, True), portions_of(amount, rows * top, limit, skew, False)
    places = jnp.arange(amount)

    def named(sizes, turn):
        used = int((sizes > 0).sum())
        fixed = max(1, used // 4)
        moved = fixed + (places - fixed + turn * (used - fixed)) % max(1, amount - fixed)
        return jnp.zeros((amount,), jnp.int32).at[order[jnp.where(places < fixed, places, moved)]].set(jnp.asarray(sizes, jnp.int32))

    sizes = jnp.where(number % 4 == 0, named(crowded, number // 4), named(common, number - number // 4 - 1))
    mixed = jax.random.permutation(jax.random.fold_in(own, 3), amount)
    donor, receiver = mixed[0:amount // 2 * 2:2], mixed[1:amount // 2 * 2:2]
    room = jnp.minimum(sizes[donor] - 1, limit - sizes[receiver]) // 2
    room = jnp.where((donor == order[0]) | (receiver == order[0]) | (sizes[receiver] == 0), 0, jnp.maximum(room, 0))
    moved = jax.random.randint(jax.random.fold_in(own, 4), (amount // 2,), 0, 1 << 20) % (room + 1)
    sizes = sizes.at[donor].add(-moved).at[receiver].add(moved)
    members = jnp.searchsorted(jnp.cumsum(sizes), jnp.arange(rows * top), side="right").astype(jnp.int32)
    listing = members.reshape(top, rows).T
    listing = listing[jax.random.permutation(jax.random.fold_in(own, 1), rows)]
    turn = jax.random.randint(jax.random.fold_in(own, 2), (rows, 1), 0, top)
    return jnp.take_along_axis(listing, (jnp.arange(top)[None, :] + turn) % top, axis=1)


def portions_of(number_of, total, reach, lean, full):
    loads = [(1 << 20) // math.isqrt(grade ** lean) + 1 for grade in range(1, number_of + 1)]
    largest = reach if full else min(reach, max(-(-total // number_of), total * loads[0] // sum(loads)))
    least = 1 if total - largest >= number_of - 1 else 0
    given, rest = [largest] + [least] * (number_of - 1), total - largest - least * (number_of - 1)
    while rest > 0:
        candidates = [i for i in range(1, number_of) if given[i] < largest] or [i for i in range(1, number_of) if given[i] < reach]
        pool, budget = sum([loads[i] for i in candidates]), rest
        for i in candidates:
            addition = min(reach - given[i], max(1, budget * loads[i] // pool), rest)
            given[i] = given[i] + addition
            rest = rest - addition
    return np.array(given)


def scatter_about(rng, extent, width, limit, shards=(), held_as=jnp.bfloat16):
    factor_of = levels(rng, extent, shards, -0.22, 0.18) if shards else 1.0
    values = jax.random.normal(rng, extent, jnp.float32) * width * factor_of
    return jnp.minimum(jnp.maximum(values, -limit), limit).astype(held_as)


def setup_inputs(seed: int = 0) -> dict:
    seeds = jax.random.split(jax.random.key(seed), 8)
    layer_inputs = scatter_about(seeds[0], (LAYERS, TOKENS, D), 1.0, 6.0, ((0, 2), (1, 32)))
    out_grad = scatter_about(seeds[1], (TOKENS, D), 1.0, 6.0, ((0, 32),))
    expert_ids_keys = jax.random.split(jax.random.fold_in(seeds[2], 1), LAYERS * TOKENS // TOK_DEV)
    expert_ids_turns = jax.random.permutation(jax.random.fold_in(seeds[2], 3), LAYERS * TOKENS // TOK_DEV)
    expert_ids = jax.vmap(lambda own, number: assign_block(jax.random.fold_in(seeds[2], 2), own, number, TOK_DEV, EXPERTS, TOP, CAP, 1))(expert_ids_keys, expert_ids_turns).reshape((LAYERS, TOKENS, TOP))
    gate_weights = jnp.clip(0.05 + 0.45 * jax.random.uniform(seeds[3], (LAYERS, TOKENS, TOP), jnp.float32) ** levels(seeds[3], (LAYERS, TOKENS, TOP), ((0, 2), (1, 32)), -0.2, 0.2), 0.05, 0.5)
    w_gate = scatter_about(seeds[4], (LAYERS, EXPERTS, D, FF), D ** -0.5, 0.125, ((0, 2), (1, 32), (3, 4)))
    w_up = scatter_about(seeds[5], (LAYERS, EXPERTS, D, FF), D ** -0.5, 0.125, ((0, 2), (1, 32), (3, 4)))
    w_down = scatter_about(seeds[6], (LAYERS, EXPERTS, FF, D), FF ** -0.5, 0.15625, ((0, 2), (1, 32), (2, 4)))
    return dict(layer_inputs=layer_inputs, out_grad=out_grad, expert_ids=expert_ids, gate_weights=gate_weights, w_gate=w_gate, w_up=w_up, w_down=w_down)


def expert_rows(table_row, gate_mat, up_mat, down_mat, input_pad, cot_pad):
    highest = lax.Precision.HIGHEST
    in_rows = jnp.take(input_pad, table_row, axis=0).astype(jnp.float32)
    cot_rows = jnp.take(cot_pad, table_row, axis=0).astype(jnp.float32)
    gate_f32 = gate_mat.astype(jnp.float32)
    up_f32 = up_mat.astype(jnp.float32)
    down_f32 = down_mat.astype(jnp.float32)
    pre_gate = jnp.dot(in_rows, gate_f32, precision=highest)
    pre_up = jnp.dot(in_rows, up_f32, precision=highest)
    hidden_grad = jnp.dot(cot_rows, down_f32.T, precision=highest)
    sig_value = jax.nn.sigmoid(pre_gate)
    gate_grad = (hidden_grad * pre_up * sig_value * (1.0 + pre_gate * (1.0 - sig_value))).astype(jnp.bfloat16)
    up_grad = (hidden_grad * pre_gate * sig_value).astype(jnp.bfloat16)
    gate_grad = lax.optimization_barrier(gate_grad).astype(jnp.float32)
    up_grad = lax.optimization_barrier(up_grad).astype(jnp.float32)
    row_count = in_rows.shape[0]
    block_width = FF // N_DP
    gate_blocks = gate_grad.reshape(row_count, N_DP, block_width)
    up_blocks = up_grad.reshape(row_count, N_DP, block_width)
    gate_wblk = gate_f32.reshape(D, N_DP, block_width)
    up_wblk = up_f32.reshape(D, N_DP, block_width)
    partial_value = jnp.einsum('mqf,dqf->qmd', gate_blocks, gate_wblk, precision=highest)
    partial_value = partial_value + jnp.einsum('mqf,dqf->qmd', up_blocks, up_wblk, precision=highest)
    partial_value = lax.optimization_barrier(partial_value.astype(jnp.bfloat16))
    return lax.optimization_barrier(jnp.sum(partial_value.astype(jnp.float32), axis=0))

def layer_grad(inputs, cotangent, route_ids, gate_vals, w_gate, w_up, w_down):
    token_total = inputs.shape[0]
    blocks = route_ids.reshape(N_EXPERT, TOK_DEV * TOP)
    hit_table = (blocks[:, :, None] == jnp.arange(EXPERTS, dtype=jnp.int32)[None, None, :]).astype(jnp.int32)
    position = lax.optimization_barrier(jnp.sum((jnp.cumsum(hit_table, axis=1) - hit_table) * hit_table, axis=2))
    source_block = jnp.arange(N_EXPERT, dtype=jnp.int32)[:, None]
    place = ((blocks * N_EXPERT + source_block) * CAP + position).reshape(-1).astype(jnp.int32)
    token_of = (jnp.arange(token_total * TOP, dtype=jnp.int32) // TOP).astype(jnp.int32)
    table = jnp.full((EXPERTS * N_EXPERT * CAP,), token_total, jnp.int32).at[place].set(token_of)
    table = table.reshape(EXPERTS, N_EXPERT * CAP)
    input_pad = jnp.concatenate([inputs, jnp.zeros((1, D), inputs.dtype)], axis=0)
    cot_pad = jnp.concatenate([cotangent, jnp.zeros((1, D), cotangent.dtype)], axis=0)

    def per_expert(pieces):
        return expert_rows(pieces[0], pieces[1], pieces[2], pieces[3], input_pad, cot_pad)
    terms = lax.map(per_expert, (table, w_gate, w_up, w_down))
    per_slot = jnp.take(terms.reshape(-1, D), place, axis=0).reshape(token_total, TOP, D)
    weighted = lax.optimization_barrier(jnp.sum(per_slot * gate_vals[:, :, None].astype(jnp.float32), axis=1))
    return (cotangent.astype(jnp.float32) + weighted).astype(jnp.bfloat16)

def reference(layer_inputs, out_grad, expert_ids, gate_weights, w_gate, w_up, w_down):
    upper = layer_grad(layer_inputs[1], out_grad, expert_ids[1], gate_weights[1], w_gate[1], w_up[1], w_down[1])
    lower = layer_grad(layer_inputs[0], upper, expert_ids[0], gate_weights[0], w_gate[0], w_up[0], w_down[0])
    return jnp.stack([lower, upper])
```

```python
import functools

import jax
import jax.numpy as jnp
from jax import lax
from jax.experimental import pallas as pl
from jax.experimental.pallas import tpu as pltpu
from jax.sharding import PartitionSpec as P

BF16 = jnp.bfloat16
F32 = jnp.float32
DIRECTIONS = 2
NT = (((1,), (1,)), ((), ()))


def dot_nn(left, right):
    return jnp.dot(left, right, preferred_element_type=F32)


def dot_nt(left, right):
    return lax.dot_general(left, right, NT, preferred_element_type=F32)


def ring_step(index, count):
    odd = index % 2
    return odd * ((index + 1) // 2) + (1 - odd) * ((count - index // 2) % count)


def kernel(
    sizes,
    x_hbm,
    g_hbm,
    ids_ref,
    gw_ref,
    wg_hbm,
    wu_hbm,
    wd_hbm,
    out_ref,
    xq,
    cq,
    res,
    posn,
    gate_of,
    xs,
    cs,
    rx,
    rc,
    wg,
    wu,
    wd,
    pre_g,
    pre_u,
    part,
    in1,
    in2,
    comb,
    ret,
    acc,
    load_sem,
    xa_send,
    xa_recv,
    ca_send,
    ca_recv,
    xy_send,
    xy_recv,
    cy_send,
    cy_recv,
    r1_send,
    r1_recv,
    r2_send,
    r2_recv,
    back_send,
    back_recv,
    hand_send,
    hand_recv,
    out_send,
    out_recv,
    go_sem,
):
    n_e, n_x, n_q, cap, top = sizes
    n_z = n_e // n_x
    local = wg.shape[0]
    tok, col = xq.shape
    rows = n_e * cap
    group_rows = n_x * cap
    half = rows // 2
    quarter = half // 2
    per_half = n_e // 2
    sec = lax.axis_index("section")
    me = lax.axis_index("expert")
    q = lax.axis_index("dp")
    z, x = me // n_x, me % n_x
    up, down, far = (q + 1) % n_q, (q + n_q - 1) % n_q, (q + 2) % n_q

    def ahead(block):
        dz, dx = ring_step(block // n_x, n_z), block % n_x
        return (z + dz) % n_z * n_x + (x + dx) % n_x

    def behind(block):
        dz, dx = ring_step(block // n_x, n_z), block % n_x
        return (z + n_z - dz) % n_z * n_x + (x + n_x - dx) % n_x

    my_cols = pl.ds(pl.multiple_of(q * col, col), col)
    loads = [
        pltpu.make_async_copy(x_hbm.at[0, :, my_cols], xq, load_sem.at[0]),
        pltpu.make_async_copy(wg_hbm.at[0], wg, load_sem.at[2]),
        pltpu.make_async_copy(wu_hbm.at[0], wu, load_sem.at[3]),
        pltpu.make_async_copy(wd_hbm.at[0], wd, load_sem.at[4]),
    ]
    load_cot = pltpu.make_async_copy(g_hbm.at[:, my_cols], cq, load_sem.at[1])
    loads[0].start()

    @pl.when(sec == 1)
    def _():
        load_cot.start()

    for copy in loads[1:]:
        copy.start()

    barrier = pltpu.get_barrier_semaphore()

    @pl.loop(1, n_e)
    def _(block):
        pl.semaphore_signal(barrier, inc=1, device_id={"expert": ahead(block)})

    for peer in (up, down, far):
        pl.semaphore_signal(barrier, inc=1, device_id={"dp": peer})
    pl.semaphore_signal(barrier, inc=1, device_id={"section": 1 - sec})

    shape = (n_e * local, tok)
    row = lax.broadcasted_iota(jnp.int32, shape, 0)
    block_of, local_of = row // local, row % local
    plane = block_of // n_x
    dz_of = jnp.where(plane % 2 == 1, (plane + 1) // 2, (n_z - plane // 2) % n_z)
    expert_of = ((z + dz_of) % n_z * n_x + (x + block_of % n_x) % n_x) * local + local_of
    named = jnp.zeros(shape, F32)
    weight = jnp.zeros(shape, F32)
    for k in range(top):
        hit = ids_ref[k : k + 1, :] == expert_of
        named = jnp.where(hit, 1.0, named)
        weight = jnp.where(hit, gw_ref[k : k + 1, :], weight)
    earlier = (
        lax.broadcasted_iota(jnp.int32, (tok, tok), 0)
        < lax.broadcasted_iota(jnp.int32, (tok, tok), 1)
    ).astype(F32)
    before = dot_nn(named.astype(BF16), earlier.astype(BF16))
    posn[...] = jnp.where(named > 0.5, before, -1.0)
    gate_of[...] = weight
    step = tok // (local * cap)

    def one_hot(i):
        pos = posn[pl.ds(pl.multiple_of(i * step * local, step * local), step * local), :]
        slot = lax.broadcasted_iota(jnp.int32, (step * local, cap, tok), 1).astype(F32)
        return jnp.where(pos[:, None, :] == slot, 1.0, 0.0)

    def pack(values, packed):
        @pl.loop(0, n_e // step)
        def _(i):
            chosen = one_hot(i).reshape(tok, tok).astype(BF16)
            picked = dot_nn(chosen, values[...]).astype(BF16)
            packed[pl.ds(i * step, step)] = picked.reshape(step, local, cap, col)

    def own_block(packed, rbuf, recv):
        return pltpu.make_async_copy(
            packed.at[0], rbuf.at[q, :, pl.ds(0, cap), :], recv.at[0]
        )

    def spread(packed, rbuf, send, recv, block):
        at = pl.ds(pl.multiple_of(block * cap, cap), cap)
        return pltpu.make_async_remote_copy(
            src_ref=packed.at[block],
            dst_ref=rbuf.at[q, :, at, :],
            send_sem=send.at[block],
            recv_sem=recv.at[block],
            device_id={"expert": ahead(block)},
        )

    def spread_all(packed, rbuf, send, recv):
        own_block(packed, rbuf, recv).start()

        @pl.loop(1, n_e)
        def _(block):
            spread(packed, rbuf, send, recv, block).start()

    def share(rbuf, send, recv, g, way):
        at = pl.ds(pl.multiple_of(g * group_rows, group_rows), group_rows)
        ref = rbuf.at[q, :, at, :]
        return pltpu.make_async_remote_copy(
            src_ref=ref,
            dst_ref=ref,
            send_sem=send.at[way, g],
            recv_sem=recv.at[way, g],
            device_id={"dp": up if way == 0 else down},
        )

    def pass_on(rbuf, send, recv, g, way):
        at = pl.ds(pl.multiple_of(g * group_rows, group_rows), group_rows)
        ref = rbuf.at[down if way == 0 else up, way, at, :]
        return pltpu.make_async_remote_copy(
            src_ref=ref,
            dst_ref=ref,
            send_sem=send.at[2 + way, g],
            recv_sem=recv.at[2 + way, g],
            device_id={"dp": up if way == 0 else down},
        )

    def gather(packed, rbuf, a_send, a_recv, y_send, y_recv):
        def arrive_and_share(g):
            @pl.loop(0, n_x)
            def _(dx):
                block = g * n_x + dx

                @pl.when(block == 0)
                def _():
                    own_block(packed, rbuf, a_recv).wait()

                @pl.when(block > 0)
                def _():
                    spread(packed, rbuf, a_send, a_recv, block).wait_recv()

            for way in range(DIRECTIONS):
                share(rbuf, y_send, y_recv, g, way).start()

        def forward(g):
            for way in range(DIRECTIONS):
                share(rbuf, y_send, y_recv, g, way).wait_recv()
                pass_on(rbuf, y_send, y_recv, g, way).start()

        @pl.loop(0, n_z + 1)
        def _(g):
            @pl.when(g < n_z)
            def _():
                arrive_and_share(g)

            @pl.when(g > 0)
            def _():
                forward(g - 1)

        @pl.loop(0, n_z)
        def _(g):
            for way in range(DIRECTIONS):
                pass_on(rbuf, y_send, y_recv, g, way).wait_recv()

    def drain(packed, rbuf, a_send, a_recv, y_send, y_recv):
        @pl.loop(1, n_e)
        def _(block):
            spread(packed, rbuf, a_send, a_recv, block).wait_send()

        @pl.loop(0, n_z)
        def _(g):
            for way in range(DIRECTIONS):
                share(rbuf, y_send, y_recv, g, way).wait_send()
                pass_on(rbuf, y_send, y_recv, g, way).wait_send()

    x_path = (xs, rx, xa_send, xa_recv)
    c_path = (cs, rc, ca_send, ca_recv)

    loads[0].wait()
    pack(xq, xs)

    @pl.when(sec == 1)
    def _():
        load_cot.wait()
        pack(cq, cs)

    pl.semaphore_wait(barrier, n_e - 1 + 3 + 1)

    def partner_go():
        pl.semaphore_signal(go_sem, inc=1, device_id={"section": 0})

    @pl.when(sec == 0)
    def _():
        pl.semaphore_wait(go_sem, 1)

    spread_all(*x_path)

    @pl.when(sec == 1)
    def _():
        spread_all(*c_path)

    gather(*x_path, xy_send, xy_recv)
    for copy in loads[1:]:
        copy.wait()

    @pl.loop(0, local * 2)
    def _(c):
        l = c // 2
        at = pl.ds(pl.multiple_of(c % 2 * half, half), half)
        for mat, pre in ((wg, pre_g), (wu, pre_u)):
            total = dot_nn(rx[0, l, at, :], mat[l, 0:col, :])
            for p in range(1, n_q):
                total += dot_nn(rx[p, l, at, :], mat[l, p * col : (p + 1) * col, :])
            pre[l, at, :] = total

    def hand_over():
        return pltpu.make_async_remote_copy(
            src_ref=res,
            dst_ref=cq,
            send_sem=hand_send,
            recv_sem=hand_recv,
            device_id={"section": 1 - sec},
        )

    @pl.when(sec == 0)
    def _():
        hand_over().wait_recv()
        pack(cq, cs)
        spread_all(*c_path)

    gather(*c_path, cy_send, cy_recv)

    @pl.when(sec == 1)
    def _():
        partner_go()

    def first_hop(l, h, way):
        at = pl.ds(pl.multiple_of(h * half + way * quarter, quarter), quarter)
        return pltpu.make_async_remote_copy(
            src_ref=part.at[2, l, at, :],
            dst_ref=in1.at[way, l, h],
            send_sem=r1_send.at[way, l, h],
            recv_sem=r1_recv.at[way, l, h],
            device_id={"dp": up if way == 0 else down},
        )

    def second_hop(l, h, way):
        at = pl.ds(pl.multiple_of(h * half, half), half)
        return pltpu.make_async_remote_copy(
            src_ref=part.at[1 if way == 0 else 3, l, at, :],
            dst_ref=in2.at[way, l, h],
            send_sem=r2_send.at[way, l, h],
            recv_sem=r2_recv.at[way, l, h],
            device_id={"dp": up if way == 0 else down},
        )

    def go_back(l, block):
        at = pl.ds(pl.multiple_of(block * cap, cap), cap)
        return pltpu.make_async_remote_copy(
            src_ref=comb.at[l, at, :],
            dst_ref=ret.at[block, l],
            send_sem=back_send.at[l, block],
            recv_sem=back_recv.at[l, block],
            device_id={"expert": behind(block)},
        )

    def stay(l):
        return pltpu.make_async_copy(
            comb.at[l, pl.ds(0, cap), :], ret.at[0, l], back_recv.at[l, 0]
        )

    def stage_compute(c):
        l, h = c // 2, c % 2
        at = pl.ds(pl.multiple_of(h * half, half), half)
        hidden = dot_nt(rc[0, l, at, :], wd[l, :, 0:col])
        for p in range(1, n_q):
            hidden += dot_nt(rc[p, l, at, :], wd[l, :, p * col : (p + 1) * col])
        gate = pre_g[l, at, :]
        sig = jax.nn.sigmoid(gate)
        gate_grad = (hidden * pre_u[l, at, :] * (sig * (1.0 + gate * (1.0 - sig)))).astype(BF16)
        up_grad = (hidden * (gate * sig)).astype(BF16)
        for d in (2, 1, 3, 0):
            cols = pl.ds(pl.multiple_of((q + d) % n_q * col, col), col)
            value = dot_nt(gate_grad, wg[l, cols, :]) + dot_nt(up_grad, wu[l, cols, :])
            part[d, l, at, :] = value.astype(BF16)
            if d == 2:
                for way in range(DIRECTIONS):
                    first_hop(l, h, way).start()

    def stage_add(c):
        l, h = c // 2, c % 2
        for way in range(DIRECTIONS):
            first_hop(l, h, way).wait_recv()
            d = 1 if way == 0 else 3
            at = pl.ds(pl.multiple_of(h * half + way * quarter, quarter), quarter)
            both = part[d, l, at, :].astype(F32) + in1[way, l, h].astype(F32)
            part[d, l, at, :] = both.astype(BF16)
            second_hop(l, h, way).start()

    def stage_back(c):
        l, h = c // 2, c % 2
        at = pl.ds(pl.multiple_of(h * half, half), half)
        for way in range(DIRECTIONS):
            second_hop(l, h, way).wait_recv()
        total = part[0, l, at, :].astype(F32) + in2[0, l, h].astype(F32)
        comb[l, at, :] = (total + in2[1, l, h].astype(F32)).astype(BF16)

        @pl.loop(0, per_half)
        def _(j):
            block = h * per_half + j

            @pl.when(block == 0)
            def _():
                stay(l).start()

            @pl.when(block > 0)
            def _():
                go_back(l, block).start()

    chunks = local * 2

    @pl.loop(0, chunks + 2)
    def _(c):
        @pl.when(c < chunks)
        def _():
            stage_compute(c)

        @pl.when(jnp.logical_and(c >= 1, c < chunks + 1))
        def _():
            stage_add(c - 1)

        @pl.when(c >= 2)
        def _():
            stage_back(c - 2)

    @pl.loop(0, local)
    def _(l):
        stay(l).wait()

        @pl.loop(1, n_e)
        def _(block):
            go_back(l, block).wait_recv()

    acc[...] = cq[...].astype(F32)

    @pl.loop(0, n_e // step)
    def _(i):
        weight = gate_of[pl.ds(pl.multiple_of(i * step * local, step * local), step * local), :]
        placed = (one_hot(i) * weight[:, None, :]).reshape(tok, tok).T
        rows_in = ret[pl.ds(i * step, step)].reshape(tok, col)
        high = placed.astype(BF16)
        rest = placed - high.astype(F32)
        middle = rest.astype(BF16)
        low = (rest - middle.astype(F32)).astype(BF16)
        acc[...] += dot_nn(high, rows_in) + (dot_nn(middle, rows_in) + dot_nn(low, rows_in))

    res[...] = acc[...].astype(BF16)

    @pl.when(sec == 1)
    def _():
        hand_over().start()

    def publish(index, peer):
        return pltpu.make_async_remote_copy(
            src_ref=res,
            dst_ref=out_ref.at[0, :, my_cols],
            send_sem=out_send.at[index],
            recv_sem=out_recv.at[index],
            device_id={"dp": peer},
        )

    shares = [publish(i, peer) for i, peer in enumerate((up, down, far))]
    for copy in shares:
        copy.start()
    out_ref[0, :, my_cols] = res[...]

    drain(*x_path, xy_send, xy_recv)
    drain(*c_path, cy_send, cy_recv)

    @pl.loop(0, local)
    def _(l):
        for h in range(2):
            for way in range(DIRECTIONS):
                first_hop(l, h, way).wait_send()
                second_hop(l, h, way).wait_send()

        @pl.loop(1, n_e)
        def _(block):
            go_back(l, block).wait_send()

    for copy in shares:
        copy.wait()

    @pl.when(sec == 1)
    def _():
        hand_over().wait_send()


def shards(n_x, layer_inputs, out_grad, expert_ids, gate_weights, w_gate, w_up, w_down):
    n_e, n_q = lax.axis_size("expert"), lax.axis_size("dp")
    _, tok, width = layer_inputs.shape
    _, local, _, hidden = w_gate.shape
    top = expert_ids.shape[2]
    cap = tok * top * 4 // (3 * local * n_e)
    col = width // n_q
    rows = n_e * cap
    n_z = n_e // n_x
    dma = pltpu.SemaphoreType.DMA
    scratch = [
        pltpu.VMEM((tok, col), BF16),
        pltpu.VMEM((tok, col), BF16),
        pltpu.VMEM((tok, col), BF16),
        pltpu.VMEM((n_e * local, tok), F32),
        pltpu.VMEM((n_e * local, tok), F32),
        pltpu.VMEM((n_e, local, cap, col), BF16),
        pltpu.VMEM((n_e, local, cap, col), BF16),
        pltpu.VMEM((n_q, local, rows, col), BF16),
        pltpu.VMEM((n_q, local, rows, col), BF16),
        pltpu.VMEM((local, width, hidden), BF16),
        pltpu.VMEM((local, width, hidden), BF16),
        pltpu.VMEM((local, hidden, width), BF16),
        pltpu.VMEM((local, rows, hidden), F32),
        pltpu.VMEM((local, rows, hidden), F32),
        pltpu.VMEM((n_q, local, rows, col), BF16),
        pltpu.VMEM((DIRECTIONS, local, 2, rows // 4, col), BF16),
        pltpu.VMEM((DIRECTIONS, local, 2, rows // 2, col), BF16),
        pltpu.VMEM((local, rows, col), BF16),
        pltpu.VMEM((n_e, local, cap, col), BF16),
        pltpu.VMEM((tok, col), F32),
        dma((5,)),
        dma((n_e,)),
        dma((n_e,)),
        dma((n_e,)),
        dma((n_e,)),
        dma((4, n_z)),
        dma((4, n_z)),
        dma((4, n_z)),
        dma((4, n_z)),
        dma((DIRECTIONS, local, 2)),
        dma((DIRECTIONS, local, 2)),
        dma((DIRECTIONS, local, 2)),
        dma((DIRECTIONS, local, 2)),
        dma((local, n_e)),
        dma((local, n_e)),
        dma,
        dma,
        dma((3,)),
        dma((3,)),
        pltpu.SemaphoreType.REGULAR,
    ]
    vmem, anywhere = pl.BlockSpec(memory_space=pltpu.VMEM), pl.BlockSpec(memory_space=pl.ANY)
    return pl.pallas_call(
        functools.partial(kernel, (n_e, n_x, n_q, cap, top)),
        out_shape=jax.ShapeDtypeStruct((1, tok, width), BF16),
        in_specs=[anywhere, anywhere, vmem, vmem, anywhere, anywhere, anywhere],
        out_specs=vmem,
        scratch_shapes=scratch,
        compiler_params=pltpu.CompilerParams(
            collective_id=0, has_side_effects=True, vmem_limit_bytes=56 * 1024 * 1024
        ),
        name="routed_input_grads",
    )(
        layer_inputs,
        out_grad,
        expert_ids[0].T,
        gate_weights[0].T,
        w_gate,
        w_up,
        w_down,
    )


def solution(mesh):
    n_x = 4 if mesh.shape["expert"] % 8 == 0 else 2
    return jax.shard_map(
        functools.partial(shards, n_x),
        mesh=mesh,
        in_specs=(
            P("section", "expert", None),
            P("expert", None),
            P("section", "expert", None),
            P("section", "expert", None),
            P("section", "expert", None, "dp"),
            P("section", "expert", None, "dp"),
            P("section", "expert", "dp", None),
        ),
        out_specs=P("section", "expert", None),
        check_vma=False,
    )
```

```python
import functools

import jax
import jax.numpy as jnp
from jax import lax
from jax.experimental import pallas as pl
from jax.experimental.pallas import tpu as pltpu
from jax.sharding import PartitionSpec as P

BF16 = jnp.bfloat16
F32 = jnp.float32
DIRECTIONS = 2
NT = (((1,), (1,)), ((), ()))
PRE_AT = 1
GO_AT = (0, 3)


def dot_nn(left, right):
    return jnp.dot(left, right, preferred_element_type=F32)


def dot_nt(left, right):
    return lax.dot_general(left, right, NT, preferred_element_type=F32)


def ring_step(index, count):
    odd = index % 2
    return odd * ((index + 1) // 2) + (1 - odd) * ((count - index // 2) % count)


def kernel(
    sizes,
    x_hbm,
    g_hbm,
    ids_ref,
    gw_ref,
    wg_hbm,
    wu_hbm,
    wd_hbm,
    out_ref,
    xq,
    cq,
    res,
    posn,
    gate_of,
    xs,
    cs,
    rx,
    rc,
    wgu,
    wd,
    pre,
    part,
    in1,
    in2,
    comb,
    ret,
    acc,
    load_sem,
    xa_send,
    xa_recv,
    ca_send,
    ca_recv,
    xy_send,
    xy_recv,
    cy_send,
    cy_recv,
    r1_send,
    r1_recv,
    r2_send,
    r2_recv,
    back_send,
    back_recv,
    hand_send,
    hand_recv,
    out_send,
    out_recv,
    go_sem,
):
    n_e, n_x, n_q, cap, top = sizes
    n_z = n_e // n_x
    local = wd.shape[0]
    hidden, padded = wd_hbm.shape[2], wd.shape[1]
    tok, col = xq.shape
    rows = n_e * cap
    group_rows = n_x * cap
    half = rows // 2
    quarter = half // 2
    per_half = n_e // 2
    sec = lax.axis_index("section")
    me = lax.axis_index("expert")
    q = lax.axis_index("dp")
    z, x = me // n_x, me % n_x
    up, down, far = (q + 1) % n_q, (q + n_q - 1) % n_q, (q + 2) % n_q

    def ahead(block):
        dz, dx = ring_step(block // n_x, n_z), block % n_x
        return (z + dz) % n_z * n_x + (x + dx) % n_x

    def behind(block):
        dz, dx = ring_step(block // n_x, n_z), block % n_x
        return (z + n_z - dz) % n_z * n_x + (x + n_x - dx) % n_x

    my_cols = pl.ds(pl.multiple_of(q * col, col), col)
    loads = [
        pltpu.make_async_copy(x_hbm.at[0, :, my_cols], xq, load_sem.at[0]),
        pltpu.make_async_copy(wg_hbm.at[0], wgu.at[:, 0:hidden, :], load_sem.at[2]),
        pltpu.make_async_copy(wu_hbm.at[0], wgu.at[:, padded : padded + hidden, :], load_sem.at[3]),
        pltpu.make_async_copy(wd_hbm.at[0], wd.at[:, 0:hidden, :], load_sem.at[4]),
    ]
    load_cot = pltpu.make_async_copy(g_hbm.at[:, my_cols], cq, load_sem.at[1])
    loads[0].start()

    @pl.when(sec == 1)
    def _():
        load_cot.start()

    for copy in loads[1:]:
        copy.start()

    barrier = pltpu.get_barrier_semaphore()

    @pl.loop(1, n_e)
    def _(block):
        pl.semaphore_signal(barrier, inc=1, device_id={"expert": ahead(block)})

    for peer in (up, down, far):
        pl.semaphore_signal(barrier, inc=1, device_id={"dp": peer})
    pl.semaphore_signal(barrier, inc=1, device_id={"section": 1 - sec})

    if padded > hidden:
        none = jnp.zeros((local, padded - hidden, wd.shape[2]), BF16)
        wgu[:, hidden:padded, :] = none
        wgu[:, padded + hidden :, :] = none
        wd[:, hidden:, :] = none

    shape = (n_e * local, tok)
    row = lax.broadcasted_iota(jnp.int32, shape, 0)
    block_of, local_of = row // local, row % local
    plane = block_of // n_x
    dz_of = jnp.where(plane % 2 == 1, (plane + 1) // 2, (n_z - plane // 2) % n_z)
    expert_of = ((z + dz_of) % n_z * n_x + (x + block_of % n_x) % n_x) * local + local_of
    named = jnp.zeros(shape, F32)
    weight = jnp.zeros(shape, F32)
    for k in range(top):
        hit = ids_ref[k] == expert_of
        named = jnp.where(hit, 1.0, named)
        weight = jnp.where(hit, gw_ref[k], weight)
    earlier = (
        lax.broadcasted_iota(jnp.int32, (tok, tok), 0)
        < lax.broadcasted_iota(jnp.int32, (tok, tok), 1)
    ).astype(F32)
    before = dot_nn(named.astype(BF16), earlier.astype(BF16))
    posn[...] = jnp.where(named > 0.5, before, -1.0)
    gate_of[...] = weight
    step = tok // (local * cap)

    def one_hot(i):
        pos = posn[pl.ds(pl.multiple_of(i * step * local, step * local), step * local), :]
        slot = lax.broadcasted_iota(jnp.int32, (step * local, cap, tok), 1).astype(F32)
        return jnp.where(pos[:, None, :] == slot, 1.0, 0.0)

    def pack(values, packed):
        @pl.loop(0, n_e // step)
        def _(i):
            chosen = one_hot(i).reshape(tok, tok).astype(BF16)
            picked = dot_nn(chosen, values[...]).astype(BF16)
            packed[pl.ds(i * step, step)] = picked.reshape(step, local, cap, col)

    def own_block(packed, rbuf, recv):
        return pltpu.make_async_copy(
            packed.at[0], rbuf.at[q, :, pl.ds(0, cap), :], recv.at[0]
        )

    def spread(packed, rbuf, send, recv, block):
        at = pl.ds(pl.multiple_of(block * cap, cap), cap)
        return pltpu.make_async_remote_copy(
            src_ref=packed.at[block],
            dst_ref=rbuf.at[q, :, at, :],
            send_sem=send.at[block],
            recv_sem=recv.at[block],
            device_id={"expert": ahead(block)},
        )

    def spread_all(packed, rbuf, send, recv):
        own_block(packed, rbuf, recv).start()

        @pl.loop(1, n_e)
        def _(block):
            spread(packed, rbuf, send, recv, block).start()

    def share(rbuf, send, recv, g, way):
        at = pl.ds(pl.multiple_of(g * group_rows, group_rows), group_rows)
        ref = rbuf.at[q, :, at, :]
        return pltpu.make_async_remote_copy(
            src_ref=ref,
            dst_ref=ref,
            send_sem=send.at[way, g],
            recv_sem=recv.at[way, g],
            device_id={"dp": up if way == 0 else down},
        )

    def pass_on(rbuf, send, recv, g, way):
        at = pl.ds(pl.multiple_of(g * group_rows, group_rows), group_rows)
        ref = rbuf.at[down if way == 0 else up, way, at, :]
        return pltpu.make_async_remote_copy(
            src_ref=ref,
            dst_ref=ref,
            send_sem=send.at[2 + way, g],
            recv_sem=recv.at[2 + way, g],
            device_id={"dp": up if way == 0 else down},
        )

    def arrive_and_share(packed, rbuf, a_send, a_recv, y_send, y_recv, g):
        @pl.loop(0, n_x)
        def _(dx):
            block = g * n_x + dx

            @pl.when(block == 0)
            def _():
                own_block(packed, rbuf, a_recv).wait()

            @pl.when(block > 0)
            def _():
                spread(packed, rbuf, a_send, a_recv, block).wait_recv()

        for way in range(DIRECTIONS):
            share(rbuf, y_send, y_recv, g, way).start()

    def forward(rbuf, y_send, y_recv, g):
        for way in range(DIRECTIONS):
            share(rbuf, y_send, y_recv, g, way).wait_recv()
            pass_on(rbuf, y_send, y_recv, g, way).start()

    def settle(rbuf, y_send, y_recv, h):
        @pl.loop(0, n_z // 2)
        def _(i):
            for way in range(DIRECTIONS):
                pass_on(rbuf, y_send, y_recv, h * (n_z // 2) + i, way).wait_recv()

    def drain(packed, rbuf, a_send, a_recv, y_send, y_recv):
        @pl.loop(1, n_e)
        def _(block):
            spread(packed, rbuf, a_send, a_recv, block).wait_send()

        @pl.loop(0, n_z)
        def _(g):
            for way in range(DIRECTIONS):
                share(rbuf, y_send, y_recv, g, way).wait_send()
                pass_on(rbuf, y_send, y_recv, g, way).wait_send()

    x_path = (xs, rx, xa_send, xa_recv)
    c_path = (cs, rc, ca_send, ca_recv)

    loads[0].wait()
    pack(xq, xs)

    @pl.when(sec == 1)
    def _():
        load_cot.wait()
        pack(cq, cs)

    pl.semaphore_wait(barrier, n_e - 1 + 3 + 1)

    x_y, c_y = (xy_send, xy_recv), (cy_send, cy_recv)

    @pl.when(sec == 0)
    def _():
        pl.semaphore_wait(go_sem.at[0], 1)

    spread_all(*x_path)

    @pl.when(sec == 1)
    def _():
        spread_all(*c_path)

    @pl.when(sec == 0)
    def _():
        pl.semaphore_wait(go_sem.at[1], 1)

    @pl.loop(0, n_z + 1)
    def _(g):
        @pl.when(g < n_z)
        def _():
            arrive_and_share(*x_path, *x_y, g)

        @pl.when(g > 0)
        def _():
            forward(rx, *x_y, g - 1)

    for copy in loads[1:]:
        copy.wait()

    chunks = local * 2

    def stage_pre(c):
        h, l = c // local, c % local

        @pl.when(l == 0)
        def _():
            settle(rx, *x_y, h)

        at = pl.ds(pl.multiple_of(h * half, half), half)
        total = dot_nt(rx[0, l, at, :], wgu[l, :, 0:col])
        for p in range(1, n_q):
            total += dot_nt(rx[p, l, at, :], wgu[l, :, p * col : (p + 1) * col])
        pre[l, at, :] = total

    def hand_over():
        return pltpu.make_async_remote_copy(
            src_ref=res,
            dst_ref=cq,
            send_sem=hand_send,
            recv_sem=hand_recv,
            device_id={"section": 1 - sec},
        )

    @pl.when(sec == 0)
    def _():
        @pl.loop(0, chunks)
        def _(c):
            stage_pre(c)

        hand_over().wait_recv()
        pack(cq, cs)
        spread_all(*c_path)

    def first_hop(l, h, way):
        at = pl.ds(pl.multiple_of(h * half + way * quarter, quarter), quarter)
        return pltpu.make_async_remote_copy(
            src_ref=part.at[2, l, at, :],
            dst_ref=in1.at[way, l, h],
            send_sem=r1_send.at[way, l, h],
            recv_sem=r1_recv.at[way, l, h],
            device_id={"dp": up if way == 0 else down},
        )

    def second_hop(l, h, way):
        at = pl.ds(pl.multiple_of(h * half, half), half)
        return pltpu.make_async_remote_copy(
            src_ref=part.at[1 if way == 0 else 3, l, at, :],
            dst_ref=in2.at[way, l, h],
            send_sem=r2_send.at[way, l, h],
            recv_sem=r2_recv.at[way, l, h],
            device_id={"dp": up if way == 0 else down},
        )

    def go_back(l, block):
        at = pl.ds(pl.multiple_of(block * cap, cap), cap)
        return pltpu.make_async_remote_copy(
            src_ref=comb.at[l, at, :],
            dst_ref=ret.at[block, l],
            send_sem=back_send.at[l, block],
            recv_sem=back_recv.at[l, block],
            device_id={"expert": behind(block)},
        )

    def stay(l):
        return pltpu.make_async_copy(
            comb.at[l, pl.ds(0, cap), :], ret.at[0, l], back_recv.at[l, 0]
        )

    def stage_compute(c):
        h, l = c // local, c % local

        @pl.when(l == 0)
        def _():
            settle(rc, *c_y, h)

        at = pl.ds(pl.multiple_of(h * half, half), half)
        hidden_grad = dot_nt(rc[0, l, at, :], wd[l, :, 0:col])
        for p in range(1, n_q):
            hidden_grad += dot_nt(rc[p, l, at, :], wd[l, :, p * col : (p + 1) * col])
        gate, up_value = pre[l, at, 0:padded], pre[l, at, padded:]
        sig = jax.nn.sigmoid(gate)
        gate_grad = (hidden_grad * up_value * (sig * (1.0 + gate * (1.0 - sig)))).astype(BF16)
        up_grad = (hidden_grad * (gate * sig)).astype(BF16)
        grads = jnp.concatenate([gate_grad, up_grad], axis=1)
        for d in (2, 1, 3, 0):
            cols = pl.ds(pl.multiple_of((q + d) % n_q * col, col), col)
            part[d, l, at, :] = dot_nn(grads, wgu[l, :, cols]).astype(BF16)
            if d == 2:
                for way in range(DIRECTIONS):
                    first_hop(l, h, way).start()

    def stage_add(c):
        h, l = c // local, c % local
        for way in range(DIRECTIONS):
            first_hop(l, h, way).wait_recv()
            d = 1 if way == 0 else 3
            at = pl.ds(pl.multiple_of(h * half + way * quarter, quarter), quarter)
            both = part[d, l, at, :].astype(F32) + in1[way, l, h].astype(F32)
            part[d, l, at, :] = both.astype(BF16)
            second_hop(l, h, way).start()

    def stage_back(c):
        h, l = c // local, c % local
        at = pl.ds(pl.multiple_of(h * half, half), half)
        for way in range(DIRECTIONS):
            second_hop(l, h, way).wait_recv()
        total = part[0, l, at, :].astype(F32) + in2[0, l, h].astype(F32)
        comb[l, at, :] = (total + in2[1, l, h].astype(F32)).astype(BF16)

        @pl.loop(0, per_half)
        def _(j):
            block = h * per_half + j

            @pl.when(block == 0)
            def _():
                stay(l).start()

            @pl.when(block > 0)
            def _():
                go_back(l, block).start()

    def within(t, low, count):
        return jnp.logical_and(t >= low, t < low + count)

    first = n_z - 1

    @pl.loop(0, first + chunks + 2)
    def _(t):
        @pl.when(t < n_z)
        def _():
            arrive_and_share(*c_path, *c_y, t)

        @pl.when(within(t, 1, n_z))
        def _():
            forward(rc, *c_y, t - 1)

        @pl.when(jnp.logical_and(sec == 1, within(t, PRE_AT, chunks)))
        def _():
            stage_pre(t - PRE_AT)

        @pl.when(jnp.logical_and(sec == 1, t == GO_AT[0]))
        def _():
            pl.semaphore_signal(go_sem.at[0], inc=1, device_id={"section": 0})

        @pl.when(within(t, first, chunks))
        def _():
            stage_compute(t - first)

        @pl.when(within(t, first + 1, chunks))
        def _():
            stage_add(t - first - 1)

        @pl.when(within(t, first + 2, chunks))
        def _():
            stage_back(t - first - 2)

        @pl.when(jnp.logical_and(sec == 1, t == first + GO_AT[1]))
        def _():
            pl.semaphore_signal(go_sem.at[1], inc=1, device_id={"section": 0})

    @pl.loop(0, local)
    def _(l):
        stay(l).wait()

        @pl.loop(1, n_e)
        def _(block):
            go_back(l, block).wait_recv()

    acc[...] = cq[...].astype(F32)

    @pl.loop(0, n_e // step)
    def _(i):
        weight = gate_of[pl.ds(pl.multiple_of(i * step * local, step * local), step * local), :]
        placed = (one_hot(i) * weight[:, None, :]).reshape(tok, tok).T
        rows_in = ret[pl.ds(i * step, step)].reshape(tok, col)
        high = placed.astype(BF16)
        rest = placed - high.astype(F32)
        middle = rest.astype(BF16)
        low = (rest - middle.astype(F32)).astype(BF16)
        acc[...] += dot_nn(high, rows_in) + (dot_nn(middle, rows_in) + dot_nn(low, rows_in))

    res[...] = acc[...].astype(BF16)

    @pl.when(sec == 1)
    def _():
        hand_over().start()

    def publish(index, peer):
        return pltpu.make_async_remote_copy(
            src_ref=res,
            dst_ref=out_ref.at[0, :, my_cols],
            send_sem=out_send.at[index],
            recv_sem=out_recv.at[index],
            device_id={"dp": peer},
        )

    shares = [publish(i, peer) for i, peer in enumerate((up, down, far))]
    for copy in shares:
        copy.start()
    out_ref[0, :, my_cols] = res[...]

    drain(*x_path, xy_send, xy_recv)
    drain(*c_path, cy_send, cy_recv)

    @pl.loop(0, local)
    def _(l):
        for h in range(2):
            for way in range(DIRECTIONS):
                first_hop(l, h, way).wait_send()
                second_hop(l, h, way).wait_send()

        @pl.loop(1, n_e)
        def _(block):
            go_back(l, block).wait_send()

    for copy in shares:
        copy.wait()

    @pl.when(sec == 1)
    def _():
        hand_over().wait_send()


def shards(n_x, layer_inputs, out_grad, expert_ids, gate_weights, w_gate, w_up, w_down):
    n_e, n_q = lax.axis_size("expert"), lax.axis_size("dp")
    _, tok, width = layer_inputs.shape
    _, local, _, hidden = w_gate.shape
    top = expert_ids.shape[2]
    cap = tok * top * 4 // (3 * local * n_e)
    col = width // n_q
    rows = n_e * cap
    n_z = n_e // n_x
    padded = -(-hidden // 128) * 128
    dma = pltpu.SemaphoreType.DMA
    scratch = [
        pltpu.VMEM((tok, col), BF16),
        pltpu.VMEM((tok, col), BF16),
        pltpu.VMEM((tok, col), BF16),
        pltpu.VMEM((n_e * local, tok), F32),
        pltpu.VMEM((n_e * local, tok), F32),
        pltpu.VMEM((n_e, local, cap, col), BF16),
        pltpu.VMEM((n_e, local, cap, col), BF16),
        pltpu.VMEM((n_q, local, rows, col), BF16),
        pltpu.VMEM((n_q, local, rows, col), BF16),
        pltpu.VMEM((local, 2 * padded, width), BF16),
        pltpu.VMEM((local, padded, width), BF16),
        pltpu.VMEM((local, rows, 2 * padded), F32),
        pltpu.VMEM((n_q, local, rows, col), BF16),
        pltpu.VMEM((DIRECTIONS, local, 2, rows // 4, col), BF16),
        pltpu.VMEM((DIRECTIONS, local, 2, rows // 2, col), BF16),
        pltpu.VMEM((local, rows, col), BF16),
        pltpu.VMEM((n_e, local, cap, col), BF16),
        pltpu.VMEM((tok, col), F32),
        dma((5,)),
        dma((n_e,)),
        dma((n_e,)),
        dma((n_e,)),
        dma((n_e,)),
        dma((4, n_z)),
        dma((4, n_z)),
        dma((4, n_z)),
        dma((4, n_z)),
        dma((DIRECTIONS, local, 2)),
        dma((DIRECTIONS, local, 2)),
        dma((DIRECTIONS, local, 2)),
        dma((DIRECTIONS, local, 2)),
        dma((local, n_e)),
        dma((local, n_e)),
        dma,
        dma,
        dma((3,)),
        dma((3,)),
        pltpu.SemaphoreType.REGULAR((2,)),
    ]
    vmem, anywhere = pl.BlockSpec(memory_space=pltpu.VMEM), pl.BlockSpec(memory_space=pl.ANY)
    return pl.pallas_call(
        functools.partial(kernel, (n_e, n_x, n_q, cap, top)),
        out_shape=jax.ShapeDtypeStruct((1, tok, width), BF16),
        in_specs=[anywhere, anywhere, vmem, vmem, anywhere, anywhere, anywhere],
        out_specs=vmem,
        scratch_shapes=scratch,
        compiler_params=pltpu.CompilerParams(
            collective_id=0, has_side_effects=True, vmem_limit_bytes=56 * 1024 * 1024
        ),
        name="routed_input_grads",
    )(
        layer_inputs,
        out_grad,
        jnp.transpose(expert_ids, (2, 0, 1)),
        jnp.transpose(gate_weights, (2, 0, 1)),
        jnp.swapaxes(w_gate, 2, 3),
        jnp.swapaxes(w_up, 2, 3),
        w_down,
    )


def solution(mesh):
    n_x = 4 if mesh.shape["expert"] % 8 == 0 else 2
    return jax.shard_map(
        functools.partial(shards, n_x),
        mesh=mesh,
        in_specs=(
            P("section", "expert", None),
            P("expert", None),
            P("section", "expert", None),
            P("section", "expert", None),
            P("section", "expert", None, "dp"),
            P("section", "expert", None, "dp"),
            P("section", "expert", "dp", None),
        ),
        out_specs=P("section", "expert", None),
        check_vma=False,
    )
```
